32 devices in a mesh: ctx: 4 (over z), head: 4 (over y, core), rep: 2 (over x).
Axes of the slice: x: 2, y: 2, z: 4, core: 2. Of those that a mesh axis runs over, the one named last changes fastest.
Arguments:
- queries: bfloat16 [4096, 1024], P(('rep', 'ctx'), 'head'), parts along dimension 0, may hold values from -140 to 140, as said below
- key_rows: bfloat16 [4096, 256], P(('rep', 'ctx')), parts along dimension 0, may hold values from -4 to 4
- value_rows: bfloat16 [4096, 256], P(('rep', 'ctx')), parts along dimension 0, may hold values from -6 to 6
- saved_output: bfloat16 [4096, 1024], P(('rep', 'ctx'), 'head'), parts along dimension 0, may hold values from -2 to 2
- out_grad: bfloat16 [4096, 1024], P(('rep', 'ctx'), 'head'), parts along dimension 0, may hold values from -6 to 6
- block_pairs: int32 [80, 2], replicated, may hold values from -1 to 15, as said below
- piece_order: int32 [8], replicated, may hold values from 0 to 7, each once
Outputs:
- query_grad: bfloat16 [4096, 1024], P(('rep', 'ctx'), 'head'), parts along dimension 0
- key_grad: float32 [4096, 256], P(('rep', 'ctx', 'head')), parts along dimension 0
- value_grad: float32 [4096, 256], P(('rep', 'ctx', 'head')), parts along dimension 0
The draws below stay inside these ranges and needn't reach their ends.
There are 2 independent parts, one for each index of `rep`. The reference program is written for one: setup_inputs(seed, part) draws one part's arguments, and reference() takes and returns one part's arrays. A program takes and returns all parts, laid end to end along the dimension named above; an argument that names none is the same for every part. Nothing has to cross between parts.
Inputs may be any that keep to these rules, and one draw needn't show every extreme that they name: `queries`: most entries are of order one; in some draws a few rows have entries up to about 60 in magnitude. `block_pairs`: each row names a query block and a key block of the 16 blocks, the key block never after the query block, or is (-1, -1) and names nothing; no pair appears twice; every query block has its diagonal pair.
All inputs are finite; a program needn't handle non-finite values.
Results may differ from the reference program's by a relative error of at most 0.0048.
Values may be sent and summed in bfloat16 or wider, within the bound.
A program may use at most 64 MiB of HBM per device.

```python
import jax
import jax.numpy as jnp
from jax import lax

HD = 128
BLOCK = 128
LOCAL = 2
GLOBAL = 1
STRIDE = 8
QH = 8
KVH = 2
SEQ = 2048
PIECE = 256
PIECES = 8
NB = 16
KPR = 5
NPAIRS = 80


def shared_rows(key):
    key_base = jax.random.truncated_normal(jax.random.fold_in(key, 17), -4.0, 4.0, (SEQ, KVH * HD), jnp.float32)
    return key_base


def draw_key_rows(key, part):
    key_base = shared_rows(key)
    return key_base.astype(jnp.bfloat16)


def draw_queries(key, part):
    drawn = jax.random.truncated_normal(jax.random.fold_in(key, 29), -4.0, 4.0, (SEQ, QH * HD), jnp.float32)
    return drawn.astype(jnp.bfloat16)


def draw_block_pairs(key, part):
    query_ids = jnp.arange(NB, dtype=jnp.int32)[:, None]
    key_ids = jnp.arange(NB, dtype=jnp.int32)[None, :]
    offset = jax.random.randint(jax.random.fold_in(key, 5), (NB, 1), 0, STRIDE)
    chosen = (key_ids <= query_ids) & ((query_ids - key_ids < LOCAL) | (key_ids < GLOBAL) | (key_ids % STRIDE == offset))
    ranking = jnp.where(chosen, key_ids, NB + key_ids)
    picked = jnp.argsort(ranking, axis=1)[:, :KPR].astype(jnp.int32)
    used = jnp.take_along_axis(chosen, picked, axis=1)
    query_col = jnp.where(used, query_ids, -1).reshape(-1)
    key_col = jnp.where(used, picked, -1).reshape(-1)
    pairs = jnp.stack([query_col, key_col], axis=1)
    shuffle = jax.random.permutation(jax.random.fold_in(key, 9), NPAIRS)
    return pairs[shuffle].astype(jnp.int32)


def shard_levels(own_key, extent, pieces, low, high):
    def one(dim, blocks):
        steps = jax.random.uniform(jax.random.fold_in(jax.random.fold_in(own_key, 6), dim), (blocks,), jnp.float32, low / len(pieces), high / len(pieces))
        return jnp.repeat(jnp.exp(steps), extent[dim] // blocks).reshape((-1,) + (1,) * (len(extent) - dim - 1))

    level = one(*pieces[0])
    for cut in pieces[1:]:
        level = level * one(*cut)
    return level


def scatter_about(stream_key, dims, spread, most, pieces=(), kind=jnp.bfloat16):
    values = jax.random.normal(stream_key, dims, jnp.float32) * spread
    if len(pieces) > 0:
        values = shard_levels(stream_key, dims, pieces, -0.22, 0.18) * values
    return jnp.clip(values, min=-most, max=most).astype(kind)


def setup_inputs(seed: int = 0, part: int = 0) -> dict:
    seeds = jax.random.split(jax.random.key(seed), 8)
    part_keys = jax.random.split(jax.random.fold_in(seeds[7], part), 8)
    queries = draw_queries(jax.random.fold_in(jax.random.fold_in(seeds[7], part), 71), part)
    key_rows = draw_key_rows(jax.random.fold_in(jax.random.fold_in(seeds[7], part), 71), part)
    value_rows = scatter_about(part_keys[2], (SEQ, KVH * HD), 1.0, 6.0, ((0, 4),))
    saved_output = scatter_about(part_keys[3], (SEQ, QH * HD), 0.3, 2.0, ((0, 4), (1, 4)))
    out_grad = scatter_about(part_keys[4], (SEQ, QH * HD), 1.0, 6.0, ((0, 4), (1, 4)))
    block_pairs = draw_block_pairs(jax.random.fold_in(seeds[7], 71), part)
    piece_order = jax.random.permutation(seeds[6], PIECES).astype(jnp.int32)
    return dict(queries=queries, key_rows=key_rows, value_rows=value_rows, saved_output=saved_output, out_grad=out_grad, block_pairs=block_pairs, piece_order=piece_order)


very_low = -1.0e30


def reference(queries, key_rows, value_rows, saved_output, out_grad, block_pairs, piece_order):
    scale_factor = HD ** -0.5
    group_size = QH // KVH
    inverse = jnp.zeros((PIECES,), jnp.int32).at[piece_order].set(jnp.arange(PIECES, dtype=jnp.int32))

    def to_sequence(array, col_count):
        return array.reshape(PIECES, PIECE, col_count)[inverse].reshape(NB, BLOCK, col_count // HD, HD)

    def to_stored(array, col_count):
        return array.reshape(PIECES, PIECE, col_count)[piece_order].reshape(SEQ, col_count)

    query_seq = to_sequence(queries, QH * HD)
    key_seq = to_sequence(key_rows, KVH * HD)
    value_seq = to_sequence(value_rows, KVH * HD)
    output_seq = to_sequence(saved_output, QH * HD)
    grad_seq = to_sequence(out_grad, QH * HD)
    within = jnp.arange(BLOCK, dtype=jnp.int32)

    def block_view(pair_row):
        query_block = jnp.maximum(pair_row[0], 0)
        key_block = jnp.maximum(pair_row[1], 0)
        allowed = (pair_row[0] >= 0) & ((key_block * BLOCK + within)[None, :] <= (query_block * BLOCK + within)[:, None])
        query_tile = query_seq[query_block].astype(jnp.float32)
        key_tile = jnp.repeat(key_seq[key_block], group_size, axis=1).astype(jnp.float32)
        scores = jnp.einsum('thd,uhd->htu', query_tile, key_tile) * scale_factor
        return query_block, key_block, allowed[None], scores, query_tile, key_tile

    def stats_step(carry, pair_row):
        run_max, run_sum = carry
        query_block, key_block, allowed, scores, query_tile, key_tile = block_view(pair_row)
        old_max = run_max[query_block]
        old_sum = run_sum[query_block]
        new_max = jnp.maximum(old_max, jnp.max(jnp.where(allowed, scores, very_low), axis=2))
        exp_terms = jnp.where(allowed, jnp.exp(scores - new_max[:, :, None]), 0.0)
        new_sum = old_sum * jnp.exp(old_max - new_max) + jnp.sum(exp_terms, axis=2)
        return (run_max.at[query_block].set(new_max), run_sum.at[query_block].set(new_sum)), None

    start_max = jnp.full((NB, QH, BLOCK), very_low, jnp.float32)
    start_sum = jnp.zeros((NB, QH, BLOCK), jnp.float32)
    (run_max, run_sum), _ = lax.scan(stats_step, (start_max, start_sum), block_pairs)
    log_sums = run_max + jnp.log(run_sum)
    delta = jnp.sum(grad_seq.astype(jnp.float32) * output_seq.astype(jnp.float32), axis=3).transpose(0, 2, 1)

    def grad_step(carry, pair_row):
        query_acc, key_acc, value_acc = carry
        query_block, key_block, allowed, scores, query_tile, key_tile = block_view(pair_row)
        attn_probs = jnp.where(allowed, jnp.exp(scores - log_sums[query_block][:, :, None]), 0.0)
        probs_low = lax.optimization_barrier(attn_probs.astype(jnp.bfloat16)).astype(jnp.float32)
        grad_tile = grad_seq[query_block].astype(jnp.float32)
        value_tile = jnp.repeat(value_seq[key_block], group_size, axis=1).astype(jnp.float32)
        dprobs = jnp.einsum('thd,uhd->htu', grad_tile, value_tile)
        dscores = attn_probs * (dprobs - delta[query_block][:, :, None])
        dscores = lax.optimization_barrier(dscores.astype(jnp.bfloat16)).astype(jnp.float32)
        query_add = scale_factor * jnp.einsum('htu,uhd->thd', dscores, key_tile)
        key_add = scale_factor * jnp.einsum('htu,thd->uhd', dscores, query_tile)
        value_add = jnp.einsum('htu,thd->uhd', probs_low, grad_tile)
        key_add = key_add.reshape(BLOCK, KVH, group_size, HD).sum(axis=2)
        value_add = value_add.reshape(BLOCK, KVH, group_size, HD).sum(axis=2)
        return (query_acc.at[query_block].add(query_add), key_acc.at[key_block].add(key_add), value_acc.at[key_block].add(value_add)), None

    start_query = jnp.zeros((NB, BLOCK, QH, HD), jnp.float32)
    start_key = jnp.zeros((NB, BLOCK, KVH, HD), jnp.float32)
    (query_acc, key_acc, value_acc), _ = lax.scan(grad_step, (start_query, start_key, start_key), block_pairs)
    query_grad = to_stored(query_acc.reshape(SEQ, QH * HD), QH * HD).astype(jnp.bfloat16)
    key_grad = to_stored(key_acc.reshape(SEQ, KVH * HD), KVH * HD)
    value_grad = to_stored(value_acc.reshape(SEQ, KVH * HD), KVH * HD)
    return (query_grad, key_grad, value_grad)
```

```python
import functools

import jax
import jax.numpy as jnp
from jax import lax
from jax.experimental import pallas as pl
from jax.experimental.pallas import tpu as pltpu
from jax.sharding import PartitionSpec as P

HD = 128
BLOCK = 128
CHUNK = 32

very_low = -1e30
far = 1e9
MESH = pl.DeviceIdType.MESH
f32 = jnp.float32
bf16 = jnp.bfloat16


def kernel(
    C, G, KV, keep,
    q_ref, k_ref, v_ref, o_ref, g_ref, pairs_ref, order_ref,
    dq_ref, dk_ref, dv_ref,
    qst, dost, kv_all, sm, dp, pb, ds_all, diff, thr, part, fromsib, comb, recv,
    zsend, zrecv, fsend, frecv, sibsend, sibrecv, rsend, rrecv,
):
    rows = q_ref.shape[0]
    heads = q_ref.shape[1] // HD
    cols = rows * heads
    half = rows // G
    H = G * KV
    piece = rows // 2
    qrow = rows // H
    blocks = rows // BLOCK
    scale = HD ** -0.5
    c = lax.axis_index("ctx")
    h = lax.axis_index("head")
    g = h // G
    s = h % G
    sib = g * G + (1 - s)

    barrier = pltpu.get_barrier_semaphore()
    for gg in range(KV):
        def hail(i, _, gg=gg):
            pl.semaphore_signal(
                barrier, inc=1,
                device_id={"ctx": (c + i) % C, "head": ((g + gg) % KV) * G + s},
                device_id_type=MESH,
            )
            return 0
        lax.fori_loop(1 if gg == 0 else 0, C, hail, 0)
    pl.semaphore_signal(barrier, inc=1, device_id={"head": sib}, device_id_type=MESH)

    gcol = pl.ds(pl.multiple_of(g * HD, HD), HD)
    for i in range(G):
        kv_all[c, 0, i] = k_ref[i * half:(i + 1) * half, gcol]
        kv_all[c, 1, i] = v_ref[i * half:(i + 1) * half, gcol]

    pl.semaphore_wait(barrier, KV * C)

    def zcopy(kind, group, to):
        return pltpu.make_async_remote_copy(
            src_ref=kv_all.at[group, kind, s], dst_ref=kv_all.at[group, kind, s],
            send_sem=zsend.at[kind * C + to], recv_sem=zrecv.at[kind * C + group],
            device_id={"ctx": to}, device_id_type=MESH,
        )

    def fcopy(kind, group, part_id):
        return pltpu.make_async_remote_copy(
            src_ref=kv_all.at[group, kind, part_id], dst_ref=kv_all.at[group, kind, part_id],
            send_sem=fsend.at[kind * C + group], recv_sem=frecv.at[kind * C + group],
            device_id={"head": sib}, device_id_type=MESH,
        )

    for kind in range(2):
        def send(i, _, kind=kind):
            zcopy(kind, c, (c + i) % C).start()
            return 0
        lax.fori_loop(1, C, send, 0)

    for i in range(heads):
        qst[i * rows:(i + 1) * rows, :] = q_ref[:, i * HD:(i + 1) * HD]
        dost[i * rows:(i + 1) * rows, :] = g_ref[:, i * HD:(i + 1) * HD]

    lane = lax.broadcasted_iota(jnp.int32, (1, cols), 1) % rows
    qblk = (
        jnp.where(lane < piece, order_ref[2 * c], order_ref[2 * c + 1]) * (piece // BLOCK)
        + (lane % piece) // BLOCK
    )
    slots = C * blocks
    per_piece = piece // BLOCK
    slot_row = lax.broadcasted_iota(jnp.int32, (1, slots), 1)
    slot_col = lax.broadcasted_iota(jnp.int32, (slots, 1), 0)
    kblk_row = jnp.zeros((1, slots), jnp.int32)
    kblk_col = jnp.zeros((slots, 1), jnp.int32)
    for i in range(2 * C):
        first = order_ref[i] * per_piece
        kblk_row = jnp.where(slot_row // per_piece == i, first + slot_row % per_piece, kblk_row)
        kblk_col = jnp.where(slot_col // per_piece == i, first + slot_col % per_piece, kblk_col)
    hits_q = (pairs_ref[:, 0:1] == qblk).astype(f32)
    hits_k = (pairs_ref[:, 1:2] == kblk_row).astype(f32)
    live = lax.dot_general(hits_k, hits_q, (((0,), (0,)), ((), ())), preferred_element_type=f32)
    thr[...] = jnp.where(
        live > 0.5,
        jnp.where(kblk_col < qblk, far, jnp.where(kblk_col == qblk, 0.0, -far)),
        -far,
    ).reshape(slots, 1, cols)
    diff[...] = (
        lax.broadcasted_iota(jnp.int32, (BLOCK, BLOCK), 0)
        - lax.broadcasted_iota(jnp.int32, (BLOCK, BLOCK), 1)
    ).astype(f32)

    delta_parts = []
    for i in range(heads):
        hc = slice(i * HD, (i + 1) * HD)
        prod = g_ref[:, hc].astype(f32) * o_ref[:, hc].astype(f32)
        delta_parts.append(jnp.sum(prod.T, axis=0, keepdims=True))
    delta = jnp.concatenate(delta_parts, axis=1)

    per_block = BLOCK // CHUNK
    chunks = rows // CHUNK
    nt = (((1,), (1,)), ((), ()))

    def scores_of(group, slot):
        sm[slot] = lax.dot_general(
            kv_all[group, 0].reshape(rows, HD), qst[...], nt, preferred_element_type=f32
        )

        def mask_chunk(i, top):
            at = pl.ds(pl.multiple_of(i * CHUNK, CHUNK), CHUNK)
            local = pl.multiple_of((i % per_block) * CHUNK, CHUNK)
            away = jnp.concatenate([diff[pl.ds(local, CHUNK), :]] * (cols // BLOCK), axis=1)
            limit = thr[group * blocks + i // per_block]
            masked = jnp.where(away <= limit, sm[slot, at, :] * scale, very_low)
            sm[slot, at, :] = masked
            return jnp.maximum(top, jnp.max(masked.reshape(CHUNK // 8, 8, cols), axis=0))

        return lax.fori_loop(
            0, chunks, mask_chunk, jnp.full((8, cols), very_low, f32), unroll=2
        )

    def slot_of(group):
        return group if keep else 0

    def stats(group, carry):
        run_max, run_sum = carry
        slot = slot_of(group)
        top = jnp.max(scores_of(group, slot), axis=0, keepdims=True)
        new_max = jnp.maximum(run_max, top)

        def sum_chunk(i, total):
            at = pl.ds(pl.multiple_of(i * CHUNK, CHUNK), CHUNK)
            terms = jnp.exp(sm[slot, at, :] - new_max)
            return total + jnp.sum(terms.reshape(CHUNK // 8, 8, cols), axis=0)

        total = lax.fori_loop(0, chunks, sum_chunk, jnp.zeros((8, cols), f32), unroll=2)
        return new_max, run_sum * jnp.exp(run_max - new_max) + jnp.sum(total, axis=0, keepdims=True)

    carry = stats(c, (jnp.full((1, cols), very_low, f32), jnp.zeros((1, cols), f32)))

    def gather_step(i, carry):
        group = (c - i + C) % C
        zcopy(0, group, c).wait_recv()
        fcopy(0, group, s).start()
        fcopy(0, group, 1 - s).wait_recv()
        return stats(group, carry)

    run_max, run_sum = lax.fori_loop(1, C, gather_step, carry)
    lse = run_max + jnp.log(run_sum)

    def forward_values(i, _):
        group = (c - i + C) % C
        zcopy(1, group, c).wait_recv()
        fcopy(1, group, s).start()
        return 0

    lax.fori_loop(1, C, forward_values, 0)

    def sib_copy(group):
        return pltpu.make_async_remote_copy(
            src_ref=part.at[group, 1 - s], dst_ref=fromsib.at[group],
            send_sem=sibsend.at[group], recv_sem=sibrecv.at[group],
            device_id={"head": sib}, device_id_type=MESH,
        )

    def out_copy(group, gg, src):
        return pltpu.make_async_remote_copy(
            src_ref=comb.at[group, gg], dst_ref=recv.at[src],
            send_sem=rsend.at[group * KV + gg], recv_sem=rrecv.at[src],
            device_id={"ctx": group, "head": gg * G + s}, device_id_type=MESH,
        )

    me = c * KV + g

    def grads(group):
        slot = slot_of(group)
        if not keep:
            scores_of(group, slot)
        dp[...] = lax.dot_general(
            kv_all[group, 1].reshape(rows, HD), dost[...], nt, preferred_element_type=f32
        )

        def chunk(i, _):
            at = pl.ds(pl.multiple_of(i * CHUNK, CHUNK), CHUNK)
            probs = jnp.exp(sm[slot, at, :] - lse)
            pb[at, :] = probs.astype(bf16)
            ds_all[group, at, :] = (probs * (dp[at, :] - delta)).astype(bf16)
            return 0

        lax.fori_loop(0, chunks, chunk, 0, unroll=2)
        dv = jnp.dot(pb[...], dost[...], preferred_element_type=f32)
        dk = jnp.dot(ds_all[group], qst[...], preferred_element_type=f32) * scale
        for hh in range(H):
            part[group, hh % G, hh // G, 0] = dk[hh * qrow:(hh + 1) * qrow, :]
            part[group, hh % G, hh // G, 1] = dv[hh * qrow:(hh + 1) * qrow, :]
        sib_copy(group).start()

    def combine(group):
        sib_copy(group).wait_recv()
        for gg in range(KV):
            comb[group, gg] = (part[group, s, gg] + fromsib[group, gg]).astype(bf16)

    def combine_and_send(group):
        combine(group)
        for gg in range(KV):
            out_copy(group, gg, me).start()

    def grad_step(i, _):
        group = (c + i) % C
        fcopy(1, group, 1 - s).wait_recv()
        grads(group)
        combine_and_send(group)
        return 0

    lax.fori_loop(1, C, grad_step, 0)
    grads(c)
    combine(c)
    others = [(g + gg) % KV for gg in range(1, KV)]
    for gg in others:
        out_copy(c, gg, me).start()

    dqt = lax.dot_general(
        kv_all[:, 0].reshape(C * rows, HD), ds_all[...].reshape(C * rows, cols),
        (((0,), (0,)), ((), ())), preferred_element_type=f32,
    ) * scale
    for i in range(heads):
        dq_ref[:, i * HD:(i + 1) * HD] = dqt[:, i * rows:(i + 1) * rows].T.astype(bf16)

    own = part[c, s, g] + fromsib[c, g]

    def collect(gg):
        def step(i, total):
            src = ((c + i) % C) * KV + gg
            out_copy(c, gg, src).wait_recv()
            return total + recv[src].astype(f32)
        return step

    sums = lax.fori_loop(1, C, collect(g), own)
    mine = pl.ds(pl.multiple_of(g * HD, HD), HD)
    dk_ref[:, mine] = sums[0]
    dv_ref[:, mine] = sums[1]
    for gg in others:
        sums = lax.fori_loop(0, C, collect(gg), jnp.zeros_like(own))
        there = pl.ds(pl.multiple_of(gg * HD, HD), HD)
        dk_ref[:, there] = sums[0]
        dv_ref[:, there] = sums[1]

    def drain(i, _):
        group = (c + i) % C
        zcopy(0, c, group).wait_send()
        zcopy(1, c, group).wait_send()
        fcopy(0, group, s).wait_send()
        fcopy(1, group, s).wait_send()
        sib_copy(group).wait_send()
        for gg in range(KV):
            out_copy(group, gg, me).wait_send()
        return 0

    lax.fori_loop(1, C, drain, 0)
    sib_copy(c).wait_send()
    for gg in others:
        out_copy(c, gg, me).wait_send()


def shards(queries, key_rows, value_rows, saved_output, out_grad, block_pairs, piece_order):
    rows, width = queries.shape
    kv_width = key_rows.shape[1]
    heads = width // HD
    C = lax.axis_size("ctx")
    H = lax.axis_size("head")
    KV = kv_width // HD
    G = H // KV
    cols = rows * heads
    qrow = rows // H
    keep = C <= 4
    vmem = pl.BlockSpec(memory_space=pltpu.VMEM)
    dma = pltpu.SemaphoreType.DMA
    return pl.pallas_call(
        functools.partial(kernel, C, G, KV, keep),
        out_shape=(
            jax.ShapeDtypeStruct((rows, width), bf16),
            jax.ShapeDtypeStruct((qrow, kv_width), f32),
            jax.ShapeDtypeStruct((qrow, kv_width), f32),
        ),
        in_specs=[vmem] * 6 + [pl.BlockSpec(memory_space=pltpu.SMEM)],
        out_specs=(vmem, vmem, vmem),
        scratch_shapes=[
            pltpu.VMEM((cols, HD), bf16),
            pltpu.VMEM((cols, HD), bf16),
            pltpu.VMEM((C, 2, G, rows // G, HD), bf16),
            pltpu.VMEM((C if keep else 1, rows, cols), f32),
            pltpu.VMEM((rows, cols), f32),
            pltpu.VMEM((rows, cols), bf16),
            pltpu.VMEM((C, rows, cols), bf16),
            pltpu.VMEM((BLOCK, BLOCK), f32),
            pltpu.VMEM((C * rows // BLOCK, 1, cols), f32),
            pltpu.VMEM((C, G, KV, 2, qrow, HD), f32),
            pltpu.VMEM((C, KV, 2, qrow, HD), f32),
            pltpu.VMEM((C, KV, 2, qrow, HD), bf16),
            pltpu.VMEM((C * KV, 2, qrow, HD), bf16),
            dma((2 * C,)), dma((2 * C,)), dma((2 * C,)), dma((2 * C,)),
            dma((C,)), dma((C,)), dma((C * KV,)), dma((C * KV,)),
        ],
        compiler_params=pltpu.CompilerParams(
            collective_id=0, has_side_effects=True, vmem_limit_bytes=56 * 1024 * 1024
        ),
    )(queries, key_rows, value_rows, saved_output, out_grad, block_pairs, piece_order)


def solution(mesh):
    placed = (
        P(("rep", "ctx"), "head"),
        P(("rep", "ctx"), None),
        P(("rep", "ctx"), None),
        P(("rep", "ctx"), "head"),
        P(("rep", "ctx"), "head"),
        P(),
        P(),
    )
    return jax.shard_map(
        shards,
        mesh=mesh,
        in_specs=placed,
        out_specs=(
            P(("rep", "ctx"), "head"),
            P(("rep", "ctx", "head"), None),
            P(("rep", "ctx", "head"), None),
        ),
        check_vma=False,
    )
```

```python
import functools

import jax
import jax.numpy as jnp
from jax import lax
from jax.experimental import pallas as pl
from jax.experimental.pallas import tpu as pltpu
from jax.sharding import PartitionSpec as P

HD = 128
BLOCK = 128
CHUNK = 32

very_low = -1e30
far = 1e9
MESH = pl.DeviceIdType.MESH
f32 = jnp.float32
bf16 = jnp.bfloat16


def kernel(
    C, G, KV, keep,
    q_ref, k_ref, v_ref, o_ref, g_ref, pairs_ref, order_ref,
    dq_ref, dk_ref, dv_ref,
    qst, dost, kv_all, sm, dp, pb, ds_all, diff, thr, part, fromsib, comb, recv,
    zsend, zrecv, fsend, frecv, sibsend, sibrecv, rsend, rrecv,
):
    rows = q_ref.shape[0]
    heads = q_ref.shape[1] // HD
    cols = rows * heads
    half = rows // G
    H = G * KV
    piece = rows // 2
    qrow = rows // H
    blocks = rows // BLOCK
    scale = HD ** -0.5
    c = lax.axis_index("ctx")
    h = lax.axis_index("head")
    g = h // G
    s = h % G
    sib = g * G + (1 - s)

    barrier = pltpu.get_barrier_semaphore()
    for gg in range(KV):
        def hail(i, _, gg=gg):
            pl.semaphore_signal(
                barrier, inc=1,
                device_id={"ctx": (c + i) % C, "head": ((g + gg) % KV) * G + s},
                device_id_type=MESH,
            )
            return 0
        lax.fori_loop(1 if gg == 0 else 0, C, hail, 0)
    pl.semaphore_signal(barrier, inc=1, device_id={"head": sib}, device_id_type=MESH)

    gcol = pl.ds(pl.multiple_of(g * HD, HD), HD)
    for i in range(G):
        kv_all[c, 0, i] = k_ref[i * half:(i + 1) * half, gcol]
        kv_all[c, 1, i] = v_ref[i * half:(i + 1) * half, gcol]

    for i in range(heads):
        qst[i * rows:(i + 1) * rows, :] = q_ref[:, i * HD:(i + 1) * HD]
        dost[i * rows:(i + 1) * rows, :] = g_ref[:, i * HD:(i + 1) * HD]

    per_piece = piece // BLOCK
    slots = C * blocks

    def stored_blocks(shape, dim, first):
        at = lax.broadcasted_iota(jnp.int32, shape, dim)
        ids = jnp.zeros(shape, jnp.int32)
        for i in range(shape[dim] // per_piece):
            ids = jnp.where(
                at // per_piece == i, order_ref[first + i] * per_piece + at % per_piece, ids
            )
        return ids

    lane = lax.broadcasted_iota(jnp.int32, (1, cols), 1) % rows
    qblk = (
        jnp.where(lane < piece, order_ref[2 * c], order_ref[2 * c + 1]) * per_piece
        + (lane % piece) // BLOCK
    )
    kblk = stored_blocks((slots, 1), 0, 0)
    own_q = stored_blocks((blocks, 1), 0, 2 * c)
    hits_q = (own_q == pairs_ref[0:1, :]).astype(f32)
    hits_k = (kblk == pairs_ref[1:2, :]).astype(f32)
    nt = (((1,), (1,)), ((), ()))
    table = lax.dot_general(hits_k, hits_q, nt, preferred_element_type=f32)
    live = jnp.concatenate(
        [jnp.broadcast_to(table[:, i:i + 1], (slots, BLOCK)) for i in range(blocks)] * heads, axis=1
    )
    thr[...] = jnp.where(
        live > 0.5, jnp.where(kblk < qblk, far, jnp.where(kblk == qblk, 0.0, -far)), -far
    ).reshape(slots, 1, cols)
    diff[...] = (
        lax.broadcasted_iota(jnp.int32, (BLOCK, BLOCK), 0)
        - lax.broadcasted_iota(jnp.int32, (BLOCK, BLOCK), 1)
    ).astype(f32)

    pl.semaphore_wait(barrier, KV * C)

    def zcopy(kind, group, to):
        return pltpu.make_async_remote_copy(
            src_ref=kv_all.at[group, kind, s], dst_ref=kv_all.at[group, kind, s],
            send_sem=zsend.at[kind * C + to], recv_sem=zrecv.at[kind * C + group],
            device_id={"ctx": to}, device_id_type=MESH,
        )

    def fcopy(kind, group, part_id):
        return pltpu.make_async_remote_copy(
            src_ref=kv_all.at[group, kind, part_id], dst_ref=kv_all.at[group, kind, part_id],
            send_sem=fsend.at[kind * C + group], recv_sem=frecv.at[kind * C + group],
            device_id={"head": sib}, device_id_type=MESH,
        )

    for kind in range(2):
        def send(i, _, kind=kind):
            zcopy(kind, c, (c + i) % C).start()
            return 0
        lax.fori_loop(1, C, send, 0)

    delta_parts = []
    for i in range(heads):
        hc = slice(i * HD, (i + 1) * HD)
        prod = g_ref[:, hc].astype(f32) * o_ref[:, hc].astype(f32)
        delta_parts.append(jnp.sum(prod.T, axis=0, keepdims=True))
    delta = jnp.concatenate(delta_parts, axis=1)

    per_block = BLOCK // CHUNK
    chunks = rows // CHUNK

    def scores_of(group, slot):
        sm[slot] = lax.dot_general(
            kv_all[group, 0].reshape(rows, HD), qst[...], nt, preferred_element_type=f32
        )

        def mask_chunk(i, top):
            at = pl.ds(pl.multiple_of(i * CHUNK, CHUNK), CHUNK)
            local = pl.multiple_of((i % per_block) * CHUNK, CHUNK)
            away = jnp.concatenate([diff[pl.ds(local, CHUNK), :]] * (cols // BLOCK), axis=1)
            limit = thr[group * blocks + i // per_block]
            masked = jnp.where(away <= limit, sm[slot, at, :] * scale, very_low)
            sm[slot, at, :] = masked
            return jnp.maximum(top, jnp.max(masked.reshape(CHUNK // 8, 8, cols), axis=0))

        return lax.fori_loop(
            0, chunks, mask_chunk, jnp.full((8, cols), very_low, f32), unroll=2
        )

    def slot_of(group):
        return group if keep else 0

    def stats(group, carry):
        run_max, run_sum = carry
        slot = slot_of(group)
        top = jnp.max(scores_of(group, slot), axis=0, keepdims=True)
        new_max = jnp.maximum(run_max, top)

        def sum_chunk(i, total):
            at = pl.ds(pl.multiple_of(i * CHUNK, CHUNK), CHUNK)
            terms = jnp.exp(sm[slot, at, :] - new_max)
            return total + jnp.sum(terms.reshape(CHUNK // 8, 8, cols), axis=0)

        total = lax.fori_loop(0, chunks, sum_chunk, jnp.zeros((8, cols), f32), unroll=2)
        return new_max, run_sum * jnp.exp(run_max - new_max) + jnp.sum(total, axis=0, keepdims=True)

    carry = stats(c, (jnp.full((1, cols), very_low, f32), jnp.zeros((1, cols), f32)))

    def gather_step(i, carry):
        group = (c - i + C) % C
        zcopy(0, group, c).wait_recv()
        fcopy(0, group, s).start()
        fcopy(0, group, 1 - s).wait_recv()
        return stats(group, carry)

    run_max, run_sum = lax.fori_loop(1, C, gather_step, carry)
    lse = run_max + jnp.log(run_sum)

    def sib_copy(kind, group):
        return pltpu.make_async_remote_copy(
            src_ref=part.at[kind, group, 1 - s], dst_ref=fromsib.at[kind, group],
            send_sem=sibsend.at[kind * C + group], recv_sem=sibrecv.at[kind * C + group],
            device_id={"head": sib}, device_id_type=MESH,
        )

    def out_copy(kind, group, gg, src):
        return pltpu.make_async_remote_copy(
            src_ref=comb.at[kind, group, gg], dst_ref=recv.at[kind, src],
            send_sem=rsend.at[(kind * C + group) * KV + gg],
            recv_sem=rrecv.at[kind * C * KV + src],
            device_id={"ctx": group, "head": gg * G + s}, device_id_type=MESH,
        )

    me = c * KV + g
    others = [(g + gg) % KV for gg in range(1, KV)]

    def share(kind, group, value):
        for hh in range(H):
            part[kind, group, hh % G, hh // G] = value[hh * qrow:(hh + 1) * qrow, :]
        sib_copy(kind, group).start()

    def combine(kind, group, own=False):
        sib_copy(kind, group).wait_recv()
        for gg in range(KV):
            comb[kind, group, gg] = (part[kind, group, s, gg] + fromsib[kind, group, gg]).astype(bf16)
        for gg in others if own else range(KV):
            out_copy(kind, group, gg, me).start()

    def value_part(group):
        slot = slot_of(group)
        if not keep:
            scores_of(group, slot)

        def chunk(i, _):
            at = pl.ds(pl.multiple_of(i * CHUNK, CHUNK), CHUNK)
            probs = jnp.exp(sm[slot, at, :] - lse)
            sm[slot, at, :] = probs
            pb[at, :] = probs.astype(bf16)
            return 0

        lax.fori_loop(0, chunks, chunk, 0, unroll=2)
        share(1, group, jnp.dot(pb[...], dost[...], preferred_element_type=f32))

    def key_part(group):
        slot = slot_of(group)
        if not keep:
            scores_of(group, slot)
        dp[...] = lax.dot_general(
            kv_all[group, 1].reshape(rows, HD), dost[...], nt, preferred_element_type=f32
        )

        def chunk(i, _):
            at = pl.ds(pl.multiple_of(i * CHUNK, CHUNK), CHUNK)
            probs = sm[slot, at, :] if keep else jnp.exp(sm[slot, at, :] - lse)
            ds_all[group, at, :] = (probs * (dp[at, :] - delta)).astype(bf16)
            return 0

        lax.fori_loop(0, chunks, chunk, 0, unroll=2)
        share(0, group, jnp.dot(ds_all[group], qst[...], preferred_element_type=f32) * scale)

    value_part(c)

    def value_step(i, _):
        arrived = (c - i + C) % C
        value_part((c + i) % C)

        @pl.when(i == 1)
        def _():
            combine(1, c, own=True)

        @pl.when(i > 1)
        def _():
            combine(1, (c + i - 1) % C)

        zcopy(1, arrived, c).wait_recv()
        fcopy(1, arrived, s).start()
        return 0

    lax.fori_loop(1, C, value_step, 0)

    def key_step(i, _):
        group = (c + i) % C
        fcopy(1, group, 1 - s).wait_recv()
        key_part(group)

        @pl.when(i == 1)
        def _():
            combine(1, (c + C - 1) % C)

        @pl.when(i > 1)
        def _():
            combine(0, (c + i - 1) % C)

        return 0

    lax.fori_loop(1, C, key_step, 0)
    key_part(c)
    combine(0, (c + C - 1) % C)

    dqt = lax.dot_general(
        kv_all[:, 0].reshape(C * rows, HD), ds_all[...].reshape(C * rows, cols),
        (((0,), (0,)), ((), ())), preferred_element_type=f32,
    ) * scale
    for i in range(heads):
        dq_ref[:, i * HD:(i + 1) * HD] = dqt[:, i * rows:(i + 1) * rows].T.astype(bf16)

    combine(0, c, own=True)

    for kind, out_ref in ((1, dv_ref), (0, dk_ref)):
        own = part[kind, c, s, g] + fromsib[kind, c, g]

        def collect(gg, kind=kind):
            def step(i, total):
                src = ((c + i) % C) * KV + gg
                out_copy(kind, c, gg, src).wait_recv()
                return total + recv[kind, src].astype(f32)
            return step

        out_ref[:, gcol] = lax.fori_loop(1, C, collect(g), own)
        for gg in others:
            there = pl.ds(pl.multiple_of(gg * HD, HD), HD)
            out_ref[:, there] = lax.fori_loop(0, C, collect(gg), jnp.zeros_like(own))

    def drain(i, _):
        group = (c + i) % C
        for kind in range(2):
            zcopy(kind, c, group).wait_send()
            fcopy(kind, group, s).wait_send()
            sib_copy(kind, group).wait_send()
            for gg in range(KV):
                out_copy(kind, group, gg, me).wait_send()
        return 0

    lax.fori_loop(1, C, drain, 0)
    for kind in range(2):
        sib_copy(kind, c).wait_send()
        for gg in others:
            out_copy(kind, c, gg, me).wait_send()


def shards(queries, key_rows, value_rows, saved_output, out_grad, block_pairs, piece_order):
    rows, width = queries.shape
    kv_width = key_rows.shape[1]
    heads = width // HD
    C = lax.axis_size("ctx")
    H = lax.axis_size("head")
    KV = kv_width // HD
    G = H // KV
    cols = rows * heads
    qrow = rows // H
    keep = C <= 4
    vmem = pl.BlockSpec(memory_space=pltpu.VMEM)
    dma = pltpu.SemaphoreType.DMA
    return pl.pallas_call(
        functools.partial(kernel, C, G, KV, keep),
        out_shape=(
            jax.ShapeDtypeStruct((rows, width), bf16),
            jax.ShapeDtypeStruct((qrow, kv_width), f32),
            jax.ShapeDtypeStruct((qrow, kv_width), f32),
        ),
        in_specs=[vmem] * 6 + [pl.BlockSpec(memory_space=pltpu.SMEM)],
        out_specs=(vmem, vmem, vmem),
        scratch_shapes=[
            pltpu.VMEM((cols, HD), bf16),
            pltpu.VMEM((cols, HD), bf16),
            pltpu.VMEM((C, 2, G, rows // G, HD), bf16),
            pltpu.VMEM((C if keep else 1, rows, cols), f32),
            pltpu.VMEM((rows, cols), f32),
            pltpu.VMEM((rows, cols), bf16),
            pltpu.VMEM((C, rows, cols), bf16),
            pltpu.VMEM((BLOCK, BLOCK), f32),
            pltpu.VMEM((C * rows // BLOCK, 1, cols), f32),
            pltpu.VMEM((2, C, G, KV, qrow, HD), f32),
            pltpu.VMEM((2, C, KV, qrow, HD), f32),
            pltpu.VMEM((2, C, KV, qrow, HD), bf16),
            pltpu.VMEM((2, C * KV, qrow, HD), bf16),
            dma((2 * C,)), dma((2 * C,)), dma((2 * C,)), dma((2 * C,)),
            dma((2 * C,)), dma((2 * C,)), dma((2 * C * KV,)), dma((2 * C * KV,)),
        ],
        compiler_params=pltpu.CompilerParams(
            collective_id=0, has_side_effects=True, vmem_limit_bytes=56 * 1024 * 1024
        ),
    )(queries, key_rows, value_rows, saved_output, out_grad, block_pairs.T, piece_order)


def solution(mesh):
    placed = (
        P(("rep", "ctx"), "head"),
        P(("rep", "ctx"), None),
        P(("rep", "ctx"), None),
        P(("rep", "ctx"), "head"),
        P(("rep", "ctx"), "head"),
        P(),
        P(),
    )
    return jax.shard_map(
        shards,
        mesh=mesh,
        in_specs=placed,
        out_specs=(
            P(("rep", "ctx"), "head"),
            P(("rep", "ctx", "head"), None),
            P(("rep", "ctx", "head"), None),
        ),
        check_vma=False,
    )
```

```python
import functools

import jax
import jax.numpy as jnp
from jax import lax
from jax.experimental import pallas as pl
from jax.experimental.pallas import tpu as pltpu
from jax.sharding import PartitionSpec as P

HD = 128
BLOCK = 128
CHUNK = 64

very_low = -1e30
far = 1e9
MESH = pl.DeviceIdType.MESH
f32 = jnp.float32
bf16 = jnp.bfloat16


def kernel(
    C, G, KV, keep,
    q_ref, k_ref, v_ref, o_ref, g_ref, pairs_ref, order_ref,
    dq_ref, dk_ref, dv_ref,
    qst, dost, kv_all, sm, dp, pb, ds_all, diff, thr, part, fromsib, comb, recv,
    zsend, zrecv, fsend, frecv, sibsend, sibrecv, rsend, rrecv,
):
    rows = q_ref.shape[0]
    heads = q_ref.shape[1] // HD
    cols = rows * heads
    half = rows // G
    H = G * KV
    piece = rows // 2
    qrow = rows // H
    blocks = rows // BLOCK
    scale = HD ** -0.5
    c = lax.axis_index("ctx")
    h = lax.axis_index("head")
    g = h // G
    s = h % G
    sib = g * G + (1 - s)

    barrier = pltpu.get_barrier_semaphore()
    for gg in range(KV):
        def hail(i, _, gg=gg):
            pl.semaphore_signal(
                barrier, inc=1,
                device_id={"ctx": (c + i) % C, "head": ((g + gg) % KV) * G + s},
                device_id_type=MESH,
            )
            return 0
        lax.fori_loop(1 if gg == 0 else 0, C, hail, 0)
    pl.semaphore_signal(barrier, inc=1, device_id={"head": sib}, device_id_type=MESH)

    gcol = pl.ds(pl.multiple_of(g * HD, HD), HD)
    for i in range(G):
        kv_all[c, 0, i] = k_ref[i * half:(i + 1) * half, gcol]
        kv_all[c, 1, i] = v_ref[i * half:(i + 1) * half, gcol]

    for i in range(heads):
        qst[i * rows:(i + 1) * rows, :] = q_ref[:, i * HD:(i + 1) * HD]
        dost[i * rows:(i + 1) * rows, :] = g_ref[:, i * HD:(i + 1) * HD]

    per_piece = piece // BLOCK
    slots = C * blocks

    def stored_blocks(shape, dim, first):
        at = lax.broadcasted_iota(jnp.int32, shape, dim)
        ids = jnp.zeros(shape, jnp.int32)
        for i in range(shape[dim] // per_piece):
            ids = jnp.where(
                at // per_piece == i, order_ref[first + i] * per_piece + at % per_piece, ids
            )
        return ids

    lane = lax.broadcasted_iota(jnp.int32, (1, cols), 1) % rows
    qblk = (
        jnp.where(lane < piece, order_ref[2 * c], order_ref[2 * c + 1]) * per_piece
        + (lane % piece) // BLOCK
    )
    kblk = stored_blocks((slots, 1), 0, 0)
    own_q = stored_blocks((blocks, 1), 0, 2 * c)
    hits_q = (own_q == pairs_ref[0:1, :]).astype(f32)
    hits_k = (kblk == pairs_ref[1:2, :]).astype(f32)
    nt = (((1,), (1,)), ((), ()))
    table = lax.dot_general(hits_k, hits_q, nt, preferred_element_type=f32)
    live = jnp.concatenate(
        [jnp.broadcast_to(table[:, i:i + 1], (slots, BLOCK)) for i in range(blocks)] * heads, axis=1
    )
    thr[...] = jnp.where(
        live > 0.5, jnp.where(kblk < qblk, far, jnp.where(kblk == qblk, 0.0, -far)), -far
    ).reshape(slots, 1, cols)
    diff[...] = (
        lax.broadcasted_iota(jnp.int32, (BLOCK, BLOCK), 0)
        - lax.broadcasted_iota(jnp.int32, (BLOCK, BLOCK), 1)
    ).astype(f32)

    pl.semaphore_wait(barrier, KV * C)

    def zcopy(kind, group, to):
        return pltpu.make_async_remote_copy(
            src_ref=kv_all.at[group, kind, s], dst_ref=kv_all.at[group, kind, s],
            send_sem=zsend.at[kind * C + to], recv_sem=zrecv.at[kind * C + group],
            device_id={"ctx": to}, device_id_type=MESH,
        )

    def fcopy(kind, group, part_id):
        return pltpu.make_async_remote_copy(
            src_ref=kv_all.at[group, kind, part_id], dst_ref=kv_all.at[group, kind, part_id],
            send_sem=fsend.at[kind * C + group], recv_sem=frecv.at[kind * C + group],
            device_id={"head": sib}, device_id_type=MESH,
        )

    for kind in range(2):
        def send(i, _, kind=kind):
            zcopy(kind, c, (c + i) % C).start()
            return 0
        lax.fori_loop(1, C, send, 0)

    delta_parts = []
    for i in range(heads):
        hc = slice(i * HD, (i + 1) * HD)
        prod = g_ref[:, hc].astype(f32) * o_ref[:, hc].astype(f32)
        delta_parts.append(jnp.sum(prod.T, axis=0, keepdims=True))
    delta = jnp.concatenate(delta_parts, axis=1)

    per_block = BLOCK // CHUNK
    chunks = rows // CHUNK

    def scores_of(group, slot):
        sm[slot] = lax.dot_general(
            kv_all[group, 0].reshape(rows, HD), qst[...], nt, preferred_element_type=f32
        )

        def mask_chunk(i, top):
            at = pl.ds(pl.multiple_of(i * CHUNK, CHUNK), CHUNK)
            local = pl.multiple_of((i % per_block) * CHUNK, CHUNK)
            away = jnp.concatenate([diff[pl.ds(local, CHUNK), :]] * (cols // BLOCK), axis=1)
            limit = thr[group * blocks + i // per_block]
            masked = jnp.where(away <= limit, sm[slot, at, :] * scale, very_low)
            sm[slot, at, :] = masked
            return jnp.maximum(top, jnp.max(masked.reshape(CHUNK // 8, 8, cols), axis=0))

        return lax.fori_loop(
            0, chunks, mask_chunk, jnp.full((8, cols), very_low, f32), unroll=2
        )

    def slot_of(group):
        return group if keep else 0

    def stats(group, carry):
        run_max, run_sum = carry
        slot = slot_of(group)
        top = jnp.max(scores_of(group, slot), axis=0, keepdims=True)
        new_max = jnp.maximum(run_max, top)

        def sum_chunk(i, total):
            at = pl.ds(pl.multiple_of(i * CHUNK, CHUNK), CHUNK)
            terms = jnp.exp(sm[slot, at, :] - new_max)
            return total + jnp.sum(terms.reshape(CHUNK // 8, 8, cols), axis=0)

        total = lax.fori_loop(0, chunks, sum_chunk, jnp.zeros((8, cols), f32), unroll=2)
        return new_max, run_sum * jnp.exp(run_max - new_max) + jnp.sum(total, axis=0, keepdims=True)

    carry = stats(c, (jnp.full((1, cols), very_low, f32), jnp.zeros((1, cols), f32)))

    def pass_on(kind, group):
        zcopy(kind, group, c).wait_recv()
        fcopy(kind, group, s).start()

    def gather_step(i, carry):
        group = (c - i + C) % C

        @pl.when(i < C - 1)
        def _():
            pass_on(0, (c - i - 1 + C) % C)

        fcopy(0, group, 1 - s).wait_recv()
        return stats(group, carry)

    pass_on(0, (c - 1 + C) % C)
    run_max, run_sum = lax.fori_loop(1, C, gather_step, carry)
    lse = run_max + jnp.log(run_sum)

    def sib_copy(kind, group):
        return pltpu.make_async_remote_copy(
            src_ref=part.at[kind, group, 1 - s], dst_ref=fromsib.at[kind, group],
            send_sem=sibsend.at[kind * C + group], recv_sem=sibrecv.at[kind * C + group],
            device_id={"head": sib}, device_id_type=MESH,
        )

    def out_copy(kind, group, gg, src):
        return pltpu.make_async_remote_copy(
            src_ref=comb.at[kind, group, gg], dst_ref=recv.at[kind, src],
            send_sem=rsend.at[(kind * C + group) * KV + gg],
            recv_sem=rrecv.at[kind * C * KV + src],
            device_id={"ctx": group, "head": gg * G + s}, device_id_type=MESH,
        )

    me = c * KV + g
    others = [(g + gg) % KV for gg in range(1, KV)]

    def share(kind, group, value):
        for hh in range(H):
            part[kind, group, hh % G, hh // G] = value[hh * qrow:(hh + 1) * qrow, :]
        sib_copy(kind, group).start()

    def combine(kind, group, own=False):
        sib_copy(kind, group).wait_recv()
        for gg in range(KV):
            comb[kind, group, gg] = (part[kind, group, s, gg] + fromsib[kind, group, gg]).astype(bf16)
        for gg in others if own else range(KV):
            out_copy(kind, group, gg, me).start()

    def value_part(group):
        slot = slot_of(group)
        if not keep:
            scores_of(group, slot)

        def chunk(i, _):
            at = pl.ds(pl.multiple_of(i * CHUNK, CHUNK), CHUNK)
            probs = jnp.exp(sm[slot, at, :] - lse)
            sm[slot, at, :] = probs
            pb[at, :] = probs.astype(bf16)
            return 0

        lax.fori_loop(0, chunks, chunk, 0, unroll=2)
        share(1, group, jnp.dot(pb[...], dost[...], preferred_element_type=f32))

    def key_part(group):
        slot = slot_of(group)
        if not keep:
            scores_of(group, slot)
        dp[...] = lax.dot_general(
            kv_all[group, 1].reshape(rows, HD), dost[...], nt, preferred_element_type=f32
        )

        def chunk(i, _):
            at = pl.ds(pl.multiple_of(i * CHUNK, CHUNK), CHUNK)
            probs = sm[slot, at, :] if keep else jnp.exp(sm[slot, at, :] - lse)
            ds_all[group, at, :] = (probs * (dp[at, :] - delta)).astype(bf16)
            return 0

        lax.fori_loop(0, chunks, chunk, 0, unroll=2)
        share(0, group, jnp.dot(ds_all[group], qst[...], preferred_element_type=f32) * scale)

    value_part(c)

    def value_step(i, _):
        arrived = (c - i + C) % C
        value_part((c + i) % C)

        @pl.when(i == 1)
        def _():
            combine(1, c, own=True)

        @pl.when(i > 1)
        def _():
            combine(1, (c + i - 1) % C)

        pass_on(1, arrived)
        return 0

    lax.fori_loop(1, C, value_step, 0)

    def key_step(i, _):
        group = (c + i) % C
        fcopy(1, group, 1 - s).wait_recv()
        key_part(group)

        @pl.when(i == 1)
        def _():
            combine(1, (c + C - 1) % C)

        @pl.when(i > 1)
        def _():
            combine(0, (c + i - 1) % C)

        return 0

    lax.fori_loop(1, C, key_step, 0)
    key_part(c)
    combine(0, (c + C - 1) % C)

    dqt = lax.dot_general(
        kv_all[:, 0].reshape(C * rows, HD), ds_all[...].reshape(C * rows, cols),
        (((0,), (0,)), ((), ())), preferred_element_type=f32,
    ) * scale
    for i in range(heads):
        dq_ref[:, i * HD:(i + 1) * HD] = dqt[:, i * rows:(i + 1) * rows].T.astype(bf16)

    combine(0, c, own=True)

    for kind, out_ref in ((1, dv_ref), (0, dk_ref)):
        own = part[kind, c, s, g] + fromsib[kind, c, g]

        def collect(gg, kind=kind):
            def step(i, total):
                src = ((c + i) % C) * KV + gg
                out_copy(kind, c, gg, src).wait_recv()
                return total + recv[kind, src].astype(f32)
            return step

        out_ref[:, gcol] = lax.fori_loop(1, C, collect(g), own)
        for gg in others:
            there = pl.ds(pl.multiple_of(gg * HD, HD), HD)
            out_ref[:, there] = lax.fori_loop(0, C, collect(gg), jnp.zeros_like(own))

    def drain(i, _):
        group = (c + i) % C
        for kind in range(2):
            zcopy(kind, c, group).wait_send()
            fcopy(kind, group, s).wait_send()
            sib_copy(kind, group).wait_send()
            for gg in range(KV):
                out_copy(kind, group, gg, me).wait_send()
        return 0

    lax.fori_loop(1, C, drain, 0)
    for kind in range(2):
        sib_copy(kind, c).wait_send()
        for gg in others:
            out_copy(kind, c, gg, me).wait_send()


def hand_over(dq_in, dk_in, dv_in, dq_ref, dk_ref, dv_ref):
    dq_ref[...] = dq_in[...]
    dk_ref[...] = dk_in[...]
    dv_ref[...] = dv_in[...]


def shards(queries, key_rows, value_rows, saved_output, out_grad, block_pairs, piece_order):
    rows, width = queries.shape
    kv_width = key_rows.shape[1]
    heads = width // HD
    C = lax.axis_size("ctx")
    H = lax.axis_size("head")
    KV = kv_width // HD
    G = H // KV
    cols = rows * heads
    qrow = rows // H
    keep = C <= 4
    vmem = pl.BlockSpec(memory_space=pltpu.VMEM)
    dma = pltpu.SemaphoreType.DMA
    grads = pl.pallas_call(
        functools.partial(kernel, C, G, KV, keep),
        out_shape=(
            jax.ShapeDtypeStruct((rows, width), bf16),
            jax.ShapeDtypeStruct((qrow, kv_width), f32),
            jax.ShapeDtypeStruct((qrow, kv_width), f32),
        ),
        in_specs=[vmem] * 6 + [pl.BlockSpec(memory_space=pltpu.SMEM)],
        out_specs=(vmem, vmem, vmem),
        scratch_shapes=[
            pltpu.VMEM((cols, HD), bf16),
            pltpu.VMEM((cols, HD), bf16),
            pltpu.VMEM((C, 2, G, rows // G, HD), bf16),
            pltpu.VMEM((C if keep else 1, rows, cols), f32),
            pltpu.VMEM((rows, cols), f32),
            pltpu.VMEM((rows, cols), bf16),
            pltpu.VMEM((C, rows, cols), bf16),
            pltpu.VMEM((BLOCK, BLOCK), f32),
            pltpu.VMEM((C * rows // BLOCK, 1, cols), f32),
            pltpu.VMEM((2, C, G, KV, qrow, HD), f32),
            pltpu.VMEM((2, C, KV, qrow, HD), f32),
            pltpu.VMEM((2, C, KV, qrow, HD), bf16),
            pltpu.VMEM((2, C * KV, qrow, HD), bf16),
            dma((2 * C,)), dma((2 * C,)), dma((2 * C,)), dma((2 * C,)),
            dma((2 * C,)), dma((2 * C,)), dma((2 * C * KV,)), dma((2 * C * KV,)),
        ],
        compiler_params=pltpu.CompilerParams(
            collective_id=0, has_side_effects=True, vmem_limit_bytes=56 * 1024 * 1024
        ),
    )(queries, key_rows, value_rows, saved_output, out_grad, block_pairs.T, piece_order)
    return pl.pallas_call(
        hand_over,
        out_shape=tuple(jax.ShapeDtypeStruct(x.shape, x.dtype) for x in grads),
        in_specs=[vmem] * 3,
        out_specs=(vmem,) * 3,
    )(*grads)


def solution(mesh):
    placed = (
        P(("rep", "ctx"), "head"),
        P(("rep", "ctx"), None),
        P(("rep", "ctx"), None),
        P(("rep", "ctx"), "head"),
        P(("rep", "ctx"), "head"),
        P(),
        P(),
    )
    return jax.shard_map(
        shards,
        mesh=mesh,
        in_specs=placed,
        out_specs=(
            P(("rep", "ctx"), "head"),
            P(("rep", "ctx", "head"), None),
            P(("rep", "ctx", "head"), None),
        ),
        check_vma=False,
    )
```
